512 devices in a mesh: grp: 16 (over z), sub: 32 (over x, y, core).
Axes of the slice: x: 4, y: 4, z: 16, core: 2. Of those that a mesh axis runs over, the one named last changes fastest.
Arguments:
- top_basis: bfloat16 [16, 512, 256], P('grp', 'sub'), may hold values from -0.375 to 0.375
- top_coeffs: bfloat16 [16, 256, 128], P('grp'), may hold values from -6 to 6
- top_coupling: float32 [16, 512, 512], P('grp')
- block_coupling: float32 [16, 32, 128, 512], P('grp', 'sub'), may hold values from -0.09375 to 0.09375
- block_basis: bfloat16 [16, 32, 128, 128], P('grp', 'sub'), may hold values from -0.5 to 0.5
- block_coeffs: bfloat16 [16, 32, 128, 128], P('grp', 'sub'), may hold values from -6 to 6
- sub_basis: bfloat16 [16, 32, 1536, 256], P('grp', 'sub'), may hold values from -0.375 to 0.375
- sub_coeffs: bfloat16 [16, 32, 256, 128], P('grp', 'sub'), may hold values from -6 to 6
- basis_widths: int32 [16, 32], P('grp', 'sub'), may hold values from 32 to 256
- constraint_modes: bfloat16 [16, 32, 1536, 512], P('grp', 'sub'), may hold values from -0.25 to 0.25
- adjacency: int32 [16, 32, 4], P('grp', 'sub'), may hold values from 0 to 4, as said below
Outputs:
- top_values: float32 [16, 512, 128], P('grp')
- block_values: bfloat16 [16, 32, 128, 128], P('grp', 'sub')
- interior: bfloat16 [16, 32, 1536, 128], P('grp', 'sub')
The draws below stay inside these ranges and needn't reach their ends.
Inputs may be any that keep to these rules, and one draw needn't show every extreme that they name: `adjacency`: the 4 entries of one substructure are different.
All inputs are finite; a program needn't handle non-finite values.
Results may differ from the reference program's by a relative error of at most 0.0044.
Values may be sent and summed in bfloat16 or wider, within the bound.
No kernel may reach another device: no remote copies, remote signals or barrier semaphores. Data moves between devices by JAX's collectives and lax.ppermute only.
A program may use at most 64 MiB of HBM per device.

```python
import math
import jax
import jax.numpy as jnp
from jax import lax

M = 128
KT = 256
KB = 128
KS = 256
NT = 512
NB = 128
ADJ = 4
NI = 1536
CHAIN = 16
N_GRP = 16
N_SUB = 32


def draw_top_coupling(key, part):
    key_speed = jax.random.fold_in(key, 11)
    key_noise = jax.random.fold_in(key, 12)
    speed = jax.random.uniform(key_speed, (N_GRP, NT), jnp.float32, 0.5, 4.0)
    diagonal = jnp.exp(math.log(0.2) / CHAIN * speed)
    identity = jnp.eye(NT, dtype=jnp.float32)[None, :, :]
    noise = jax.random.normal(key_noise, (N_GRP, NT, NT), jnp.float32) * (0.2 / math.sqrt(NT))
    return identity * diagonal[:, :, None] + noise


def draw_basis_widths(key, part):
    key_width = jax.random.fold_in(key, 21)
    key_high = jax.random.fold_in(key, 22)
    key_low = jax.random.fold_in(key, 23)
    widths = jax.random.randint(key_width, (N_GRP * N_SUB,), KS // 8, KS + 1)
    high_pick = jax.random.randint(key_high, (), 0, N_GRP * N_SUB)
    low_pick = (high_pick + 1 + jax.random.randint(key_low, (), 0, N_GRP * N_SUB - 1)) % (N_GRP * N_SUB)
    places = jnp.arange(N_GRP * N_SUB)
    widths = jnp.where(places == high_pick, KS, widths)
    widths = jnp.where(places == low_pick, KS // 8, widths)
    return widths.reshape(N_GRP, N_SUB).astype(jnp.int32)


def draw_adjacency(key, part):
    key_order = jax.random.fold_in(key, 31)
    scores = jax.random.randint(key_order, (N_GRP, N_SUB, 5), 0, 1 << 20) * 8 + jnp.arange(5)
    order = jnp.argsort(scores, axis=-1)
    return order[..., :ADJ].astype(jnp.int32)


def level_of(stream_key, shape, cuts, low, top_value):
    loudness, own = 1.0, jax.random.fold_in(stream_key, 6)
    for dim, blocks in cuts:
        steps = jnp.exp(jax.random.uniform(jax.random.fold_in(own, dim), (blocks,), jnp.float32, low / len(cuts), top_value / len(cuts)))
        loudness = loudness * jnp.repeat(steps, shape[dim] // blocks).reshape([-1 if axis == dim else 1 for axis in range(len(shape))])
    return loudness


def centred(stream_key, dims, scale, reach, cuts=(), kind=jnp.bfloat16):
    factor_of = level_of(stream_key, dims, cuts, -0.22, 0.18) if cuts else 1.0
    drawn = jax.random.normal(stream_key, dims, jnp.float32) * scale * factor_of
    return jnp.minimum(jnp.maximum(drawn, -reach), reach).astype(kind)


def setup_inputs(seed: int = 0) -> dict:
    keys = jax.random.split(jax.random.key(seed), 12)
    top_basis = centred(keys[0], (N_GRP, NT, KT), KT ** -0.5, 0.375, ((0, 16), (1, 32)))
    top_coeffs = centred(keys[1], (N_GRP, KT, M), 1.0, 6.0, ((0, 16),))
    top_coupling = draw_top_coupling(jax.random.fold_in(keys[11], 71), 0)
    block_coupling = centred(keys[3], (N_GRP, N_SUB, NB, NT), (8 * NT) ** -0.5, 0.09375, ((0, 16), (1, 32)), jnp.float32)
    block_basis = centred(keys[4], (N_GRP, N_SUB, NB, KB), KB ** -0.5, 0.5, ((0, 16), (1, 32)))
    block_coeffs = centred(keys[5], (N_GRP, N_SUB, KB, M), 1.0, 6.0, ((0, 16), (1, 32)))
    sub_basis = centred(keys[6], (N_GRP, N_SUB, NI, KS), KS ** -0.5, 0.375, ((0, 16), (1, 32)))
    sub_coeffs = centred(keys[7], (N_GRP, N_SUB, KS, M), 1.0, 6.0, ((0, 16), (1, 32)))
    basis_widths = draw_basis_widths(jax.random.fold_in(keys[11], 71), 0)
    constraint_modes = centred(keys[9], (N_GRP, N_SUB, NI, ADJ * NB), (ADJ * NB) ** -0.5, 0.25, ((0, 16), (1, 32)))
    adjacency = draw_adjacency(jax.random.fold_in(keys[11], 71), 0)
    return dict(top_basis=top_basis, top_coeffs=top_coeffs, top_coupling=top_coupling, block_coupling=block_coupling, block_basis=block_basis, block_coeffs=block_coeffs, sub_basis=sub_basis, sub_coeffs=sub_coeffs, basis_widths=basis_widths, constraint_modes=constraint_modes, adjacency=adjacency)


def chain_turn(previous, pieces):
    coupling_now, own_now = pieces
    current = own_now + jnp.dot(coupling_now, previous, precision=lax.Precision.HIGHEST)
    return current, current


def group_interior(pieces):
    basis, coeffs, widths_here, modes, slots, blocks = pieces
    live_mask = lax.broadcasted_iota(jnp.int32, (1, KS, 1), 1) < widths_here[:, None, None]
    live_coeffs = jnp.where(live_mask, coeffs, jnp.zeros_like(coeffs))
    fixed_part = jnp.einsum("sik,skm->sim", basis.astype(jnp.float32), live_coeffs.astype(jnp.float32))
    places = jnp.arange(N_SUB, dtype=jnp.int32)[:, None]
    neighbour = (places + slots - 2) % N_SUB
    chosen = blocks[neighbour]
    linked = chosen.reshape(N_SUB, ADJ * NB, M).astype(jnp.float32)
    bound_part = jnp.einsum("sir,srm->sim", modes.astype(jnp.float32), linked)
    return (fixed_part + bound_part).astype(jnp.bfloat16)


def reference(top_basis, top_coeffs, top_coupling, block_coupling, block_basis, block_coeffs, sub_basis, sub_coeffs, basis_widths, constraint_modes, adjacency):
    top_own = jnp.einsum("gnk,gkm->gnm", top_basis.astype(jnp.float32), top_coeffs.astype(jnp.float32))
    start_value = jnp.zeros((NT, M), jnp.float32)
    unused, top_values = lax.scan(chain_turn, start_value, (top_coupling, top_own))
    own_block = jnp.einsum("gsnk,gskm->gsnm", block_basis.astype(jnp.float32), block_coeffs.astype(jnp.float32))
    from_top = jnp.einsum("gsnt,gtm->gsnm", block_coupling, top_values, precision=lax.Precision.HIGHEST)
    block_values = (own_block + from_top).astype(jnp.bfloat16)
    interior = lax.map(group_interior, (sub_basis, sub_coeffs, basis_widths, constraint_modes, adjacency, block_values))
    return top_values, block_values, interior
```

```python
import jax
import jax.numpy as jnp
from jax import lax
from jax.sharding import PartitionSpec as P

BF16 = jnp.bfloat16
F32 = jnp.float32
WINDOW = 3


def split(value):
    high = lax.reduce_precision(value, 8, 7)
    return high.astype(BF16), (value - high).astype(BF16)


def spread(piece):
    peers = lax.axis_size("sub")
    copies = jnp.broadcast_to(piece[None], (peers,) + piece.shape)
    return lax.all_to_all(copies, "sub", 0, 0)


def along_chain(value, by, groups):
    peers = lax.axis_size("sub")
    pairs = [((g - by) * peers + s, g * peers + s) for g in groups if g >= by for s in range(1, peers, 2)]
    return lax.ppermute(value, ("grp", "sub"), pairs)


def along_loop(value, by):
    peers = lax.axis_size("sub")
    return lax.ppermute(value, "sub", [(i, (i + by) % peers) for i in range(peers)])


def times(left, right):
    dims = (((1,), (1,)), ((), ()))
    high, low = left
    return lax.dot_general(right, high, dims, preferred_element_type=F32) + lax.dot_general(
        right, low, dims, preferred_element_type=F32
    )


def rows_times(value, left):
    dims = (((1,), (1,)), ((), ()))
    return lax.dot_general(value, left, dims, precision=lax.Precision.HIGH, preferred_element_type=F32)


def body(
    top_basis,
    top_coeffs,
    top_coupling,
    block_coupling,
    block_basis,
    block_coeffs,
    sub_basis,
    sub_coeffs,
    basis_widths,
    constraint_modes,
    adjacency,
):
    chain = lax.axis_size("grp")
    place = lax.axis_index("sub")
    coupling = top_coupling[0]
    high, low = split(coupling)

    back_1 = along_chain(high, 1, range(2, chain))
    back_2 = along_chain(high, 2, range(3, chain))
    basis = spread(top_basis[0]).reshape(-1, top_basis.shape[-1])

    columns = top_coeffs.shape[-1] * 2 // lax.axis_size("sub")
    coeffs = lax.dynamic_slice_in_dim(top_coeffs[0].T, (place // 2) * columns, columns, 0)
    own = lax.dot_general(coeffs, basis, (((1,), (1,)), ((), ())), preferred_element_type=F32)

    two = jnp.dot(high, back_1, preferred_element_type=F32) + jnp.dot(low, back_1, preferred_element_type=F32)
    two_high, two_low = split(two)
    three = jnp.dot(two_high, back_2, preferred_element_type=F32) + jnp.dot(two_low, back_2, preferred_element_type=F32)

    own_1 = along_chain(own, 1, range(1, chain))
    own_2 = along_chain(own, 2, range(2, chain))
    field = own + rows_times(own_1, coupling) + rows_times(own_2, two)
    for first in range(WINDOW, chain, WINDOW):
        earlier = along_chain(field, WINDOW, range(first, min(first + WINDOW, chain)))
        field = field + rows_times(earlier, three)

    pieces = spread(field.astype(BF16))
    whole = pieces.reshape(-1, 2, columns, pieces.shape[-1])[:, 1].reshape(-1, pieces.shape[-1])
    top_field = whole.astype(F32).T

    own_block = jnp.dot(block_basis[0, 0], block_coeffs[0, 0], preferred_element_type=F32)
    nt = (((1,), (1,)), ((), ()))
    from_top = lax.dot_general(block_coupling[0, 0].astype(BF16), whole, nt, preferred_element_type=F32)
    block = (own_block + from_top).astype(BF16)
    records = [along_loop(block, -offset) if offset else block for offset in (-2, -1, 0, 1, 2)]
    candidates = jnp.stack(records)
    slots = adjacency[0, 0]
    chosen = jnp.take(candidates, slots, axis=0)
    linked = chosen.reshape(slots.shape[0] * block.shape[0], block.shape[1])
    bound_part = jnp.dot(constraint_modes[0, 0], linked, preferred_element_type=F32)
    coeffs = sub_coeffs[0, 0]
    live_mask = lax.broadcasted_iota(jnp.int32, (coeffs.shape[0], 1), 0) < basis_widths[0, 0]
    live_coeffs = jnp.where(live_mask, coeffs, jnp.zeros_like(coeffs))
    fixed_part = jnp.dot(sub_basis[0, 0], live_coeffs, preferred_element_type=F32)
    interior = (fixed_part + bound_part).astype(BF16)
    return (top_field[None], block[None, None], interior[None, None])


def solution(mesh):
    placed = (
        P("grp", "sub", None),
        P("grp", None, None),
        P("grp", None, None),
        P("grp", "sub", None, None),
        P("grp", "sub", None, None),
        P("grp", "sub", None, None),
        P("grp", "sub", None, None),
        P("grp", "sub", None, None),
        P("grp", "sub"),
        P("grp", "sub", None, None),
        P("grp", "sub", None),
    )
    return jax.shard_map(
        body,
        mesh=mesh,
        in_specs=placed,
        out_specs=(P("grp", None, None), P("grp", "sub", None, None), P("grp", "sub", None, None)),
        check_vma=False,
    )
```

```python
import jax
import jax.numpy as jnp
from jax import lax
from jax.experimental import pallas as pl
from jax.experimental.pallas import tpu as pltpu
from jax.sharding import PartitionSpec as P


BF16 = jnp.bfloat16
F32 = jnp.float32
HALF = 8
PARTS = 2


def split(value):
    high = lax.reduce_precision(value, 8, 7)
    return high.astype(BF16), (value - high).astype(BF16)


def spread(piece, parts=1):
    peers = lax.axis_size("sub") // parts
    copies = jnp.broadcast_to(piece[None], (peers,) + piece.shape)
    groups = [list(range(part * peers, (part + 1) * peers)) for part in range(parts)]
    return lax.all_to_all(copies, "sub", 0, 0, axis_index_groups=groups if parts > 1 else None)


def along_chain(value, by, groups):
    peers = lax.axis_size("sub")
    pairs = [((g - by) * peers + s, g * peers + s) for g in groups if g >= by for s in range(1, peers, 2)]
    return lax.ppermute(value, ("grp", "sub"), pairs)


def swap_cores(value):
    peers = lax.axis_size("sub")
    return lax.ppermute(value, "sub", [(i, i ^ 1) for i in range(peers)])


def even_along_loop(value, by):
    peers = lax.axis_size("sub")
    return lax.ppermute(value, "sub", [(i, (i + by) % peers) for i in range(0, peers, 2)])


def even_to_odd(value):
    peers = lax.axis_size("sub")
    return lax.ppermute(value, "sub", [(i, i + 1) for i in range(0, peers, 2)])


def rows_times(value, left):
    dims = (((1,), (1,)), ((), ()))
    return lax.dot_general(value, left, dims, precision=lax.Precision.HIGH, preferred_element_type=F32)


ROWS = 256


def prepare_kernel(picks, mine, partner, before, after, returned, modes, basis, coeffs, weight, fixed, linked):
    size = mine.shape[0]
    length = weight.shape[1]
    parity = picks[5]
    for slot in range(4):
        pick = picks[slot]
        rows = pl.ds(slot * size, size)

        @pl.when(pick < 2)
        def _():
            linked[rows, :] = before[pick] + returned[pick]

        @pl.when(pick == parity + 2)
        def _():
            linked[rows, :] = mine[...]

        @pl.when(pick == 3 - parity)
        def _():
            linked[rows, :] = partner[...]

        @pl.when(pick > 3)
        def _():
            linked[rows, :] = after[pick - 4] + returned[pick - 2]

    live = lax.broadcasted_iota(jnp.int32, coeffs.shape, 0) < picks[4]
    kept = jnp.where(live, coeffs[...], jnp.zeros(coeffs.shape, coeffs.dtype))

    @pl.loop(0, modes.shape[0] // ROWS)
    def _(step):
        rows = pl.ds(pl.multiple_of(step * ROWS, ROWS), ROWS)
        both = jnp.dot(modes[rows, :], linked[...], preferred_element_type=F32)
        weight[rows, :] = both[:, :length].astype(BF16)
        fixed[rows, :] = both[:, length:] + jnp.dot(basis[rows, :], kept, preferred_element_type=F32)


def prepare(picks, mine, partner, before, after, returned, modes, basis, coeffs):
    vmem = pl.BlockSpec(memory_space=pltpu.VMEM)
    points, depth = modes.shape
    columns = coeffs.shape[1]
    length = mine.shape[1] - columns
    return pl.pallas_call(
        prepare_kernel,
        out_shape=(jax.ShapeDtypeStruct((points, length), BF16), jax.ShapeDtypeStruct((points, columns), F32)),
        in_specs=[pl.BlockSpec(memory_space=pltpu.SMEM)] + [vmem] * 8,
        out_specs=(vmem, vmem),
        scratch_shapes=[pltpu.VMEM((depth, mine.shape[1]), BF16)],
        compiler_params=pltpu.CompilerParams(vmem_limit_bytes=24 << 20),
        cost_estimate=pl.CostEstimate(flops=1_200_000_000, bytes_accessed=7_000_000, transcendentals=0),
    )(picks, mine, partner, before, after, returned, modes, basis, coeffs)


def close_kernel(pieces, coupling, own, weight, fixed, top, block, interior):
    chips, _, columns, length = pieces.shape
    field = pieces[:, 1].reshape(chips * columns, length).astype(F32).T
    top[...] = field
    rounded = field.astype(BF16)
    block[...] = (own[...] + jnp.dot(coupling[...], rounded, preferred_element_type=F32)).astype(BF16)

    @pl.loop(0, weight.shape[0] // ROWS)
    def _(step):
        rows = pl.ds(pl.multiple_of(step * ROWS, ROWS), ROWS)
        part = jnp.dot(weight[rows, :], rounded, preferred_element_type=F32)
        interior[rows, :] = (fixed[rows, :] + part).astype(BF16)


def close(pieces, coupling, own_block, weight, fixed):
    members, columns, length = pieces.shape
    vmem = pl.BlockSpec(memory_space=pltpu.VMEM)
    return pl.pallas_call(
        close_kernel,
        out_shape=(
            jax.ShapeDtypeStruct((length, members // 2 * columns), F32),
            jax.ShapeDtypeStruct(own_block.shape, BF16),
            jax.ShapeDtypeStruct(fixed.shape, BF16),
        ),
        in_specs=[vmem] * 5,
        out_specs=(vmem, vmem, vmem),
        compiler_params=pltpu.CompilerParams(vmem_limit_bytes=24 << 20),
        cost_estimate=pl.CostEstimate(flops=230_000_000, bytes_accessed=4_000_000, transcendentals=0),
    )(pieces.reshape(members // 2, 2, columns, length), coupling, own_block, weight, fixed)


def body(
    top_basis,
    top_coeffs,
    top_coupling,
    block_coupling,
    block_basis,
    block_coeffs,
    sub_basis,
    sub_coeffs,
    basis_widths,
    constraint_modes,
    adjacency,
):
    chain = lax.axis_size("grp")
    place = lax.axis_index("sub")
    coupling = top_coupling[0]
    high, low = split(coupling)

    basis = spread(top_basis[0]).reshape(-1, top_basis.shape[-1])
    back_1 = along_chain(high, 1, range(2, chain))

    chips = lax.axis_size("sub") // (2 * PARTS)
    columns = top_coeffs.shape[-1] // chips
    coeffs = lax.dynamic_slice_in_dim(top_coeffs[0].T, (place // 2 % chips) * columns, columns, 0)
    own = lax.dot_general(coeffs, basis, (((1,), (1,)), ((), ())), preferred_element_type=F32)

    own_1 = along_chain(own, 1, range(1, chain))
    two = jnp.dot(high, back_1, preferred_element_type=F32) + jnp.dot(low, back_1, preferred_element_type=F32)
    two_high, two_low = split(two)
    field = own + rows_times(own_1, coupling)

    back_2 = along_chain(two_high, 2, range(HALF, chain))
    late_2 = along_chain(field, 2, range(HALF, chain))
    for first in range(2, HALF, 2):
        earlier = along_chain(field, 2, range(first, first + 2))
        field = field + rows_times(earlier, two)
    field = field + rows_times(late_2, two)
    four = jnp.dot(two_high, back_2, preferred_element_type=F32) + jnp.dot(two_low, back_2, preferred_element_type=F32)
    for first in range(HALF, chain, 4):
        earlier = along_chain(field, 4, range(first, first + 4))
        field = field + rows_times(earlier, four)

    pieces = spread(field.astype(BF16), PARTS)

    own_block = jnp.dot(block_basis[0, 0], block_coeffs[0, 0], preferred_element_type=F32)
    block_high = block_coupling[0, 0].astype(BF16)
    mine = jnp.concatenate([block_high, own_block.astype(BF16)], axis=1)
    partner = swap_cores(mine)
    pair = jnp.stack([mine, partner])
    before = even_along_loop(pair, 2)
    after = even_along_loop(pair, -2)
    both = jnp.concatenate([before, after])
    returned = even_to_odd(both)
    parity = place % 2
    picks = jnp.concatenate([adjacency[0, 0] + parity, basis_widths[0], parity[None]]).astype(jnp.int32)
    weight, fixed = prepare(
        picks,
        mine,
        partner,
        before,
        after,
        returned,
        constraint_modes[0, 0],
        sub_basis[0, 0],
        sub_coeffs[0, 0],
    )
    top_field, block, interior = close(pieces, block_high, own_block, weight, fixed)
    return (top_field[None], block[None, None], interior[None, None])


def solution(mesh):
    placed = (
        P("grp", "sub", None),
        P("grp", None, None),
        P("grp", None, None),
        P("grp", "sub", None, None),
        P("grp", "sub", None, None),
        P("grp", "sub", None, None),
        P("grp", "sub", None, None),
        P("grp", "sub", None, None),
        P("grp", "sub"),
        P("grp", "sub", None, None),
        P("grp", "sub", None),
    )

    return jax.shard_map(
        body,
        mesh=mesh,
        in_specs=placed,
        out_specs=(P("grp", None, None), P("grp", "sub", None, None), P("grp", "sub", None, None)),
        check_vma=False,
    )
```

```python
import functools

import jax
import jax.numpy as jnp
from jax import lax
from jax.experimental import pallas as pl
from jax.experimental.pallas import tpu as pltpu
from jax.sharding import PartitionSpec as P


BF16 = jnp.bfloat16
F32 = jnp.float32
ROWS = 256
LATE = 10
LAST = 12
PARTS = 2


def spread(piece, parts=1):
    peers = lax.axis_size("sub") // parts
    copies = jnp.broadcast_to(piece[None], (peers,) + piece.shape)
    groups = [list(range(part * peers, (part + 1) * peers)) for part in range(parts)]
    return lax.all_to_all(copies, "sub", 0, 0, axis_index_groups=groups if parts > 1 else None)


def along_chain(value, by, groups):
    peers = lax.axis_size("sub")
    pairs = [((g - by) * peers + s, g * peers + s) for g in groups if g >= by for s in range(1, peers, 2)]
    return lax.ppermute(value, ("grp", "sub"), pairs)


def swap_cores(value):
    peers = lax.axis_size("sub")
    return lax.ppermute(value, "sub", [(i, i ^ 1) for i in range(peers)])


def even_along_loop(value, by):
    peers = lax.axis_size("sub")
    return lax.ppermute(value, "sub", [(i, (i + by) % peers) for i in range(0, peers, 2)])


def even_to_odd(value):
    peers = lax.axis_size("sub")
    return lax.ppermute(value, "sub", [(i, i + 1) for i in range(0, peers, 2)])


def advance_kernel(first, last, left, right, product, *rounded):
    steps = left.shape[0] // ROWS
    if first:
        group = lax.axis_index("grp")
        used = (group >= first) & (group < last)

        @pl.when(jnp.logical_not(used))
        def _():
            product[...] = jnp.zeros(product.shape, F32)

        steps = jnp.where(used, steps, 0)

    @pl.loop(0, steps)
    def _(step):
        rows = pl.ds(pl.multiple_of(step * ROWS, ROWS), ROWS)
        whole = left[rows, :]
        high = whole.astype(BF16)
        low = (whole - high.astype(F32)).astype(BF16)
        result = jnp.dot(high, right[...], preferred_element_type=F32)
        result = result + jnp.dot(low, right[...], preferred_element_type=F32)
        product[rows, :] = result
        for out in rounded:
            out[rows, :] = result.astype(BF16)


def advance(left, right, copies, first, last):
    vmem = pl.BlockSpec(memory_space=pltpu.VMEM)
    return pl.pallas_call(
        functools.partial(advance_kernel, first, last),
        out_shape=[jax.ShapeDtypeStruct(left.shape, F32)] + [jax.ShapeDtypeStruct(left.shape, BF16)] * copies,
        in_specs=[vmem] * 2,
        out_specs=[vmem] * (1 + copies),
        compiler_params=pltpu.CompilerParams(vmem_limit_bytes=8 << 20),
        cost_estimate=pl.CostEstimate(flops=540_000_000, bytes_accessed=3_000_000, transcendentals=0),
    )(left, right)


def rows_times(value, left):
    dims = (((1,), (1,)), ((), ()))
    return lax.dot_general(value, left, dims, precision=lax.Precision.HIGH, preferred_element_type=F32)


def prepare_kernel(picks, mine, partner, before, after, returned, modes, basis, coeffs, weight, fixed, linked):
    size = mine.shape[0]
    length = weight.shape[1]
    parity = picks[5]
    for slot in range(4):
        pick = picks[slot]
        rows = pl.ds(slot * size, size)

        @pl.when(pick < 2)
        def _():
            linked[rows, :] = before[pick] + returned[pick]

        @pl.when(pick == parity + 2)
        def _():
            linked[rows, :] = mine[...]

        @pl.when(pick == 3 - parity)
        def _():
            linked[rows, :] = partner[...]

        @pl.when(pick > 3)
        def _():
            linked[rows, :] = after[pick - 4] + returned[pick - 2]

    live = lax.broadcasted_iota(jnp.int32, coeffs.shape, 0) < picks[4]
    kept = jnp.where(live, coeffs[...], jnp.zeros(coeffs.shape, coeffs.dtype))

    @pl.loop(0, modes.shape[0] // ROWS)
    def _(step):
        rows = pl.ds(pl.multiple_of(step * ROWS, ROWS), ROWS)
        both = jnp.dot(modes[rows, :], linked[...], preferred_element_type=F32)
        weight[rows, :] = both[:, :length].astype(BF16)
        fixed[rows, :] = both[:, length:] + jnp.dot(basis[rows, :], kept, preferred_element_type=F32)


def prepare(picks, mine, partner, before, after, returned, modes, basis, coeffs):
    vmem = pl.BlockSpec(memory_space=pltpu.VMEM)
    points, depth = modes.shape
    columns = coeffs.shape[1]
    length = mine.shape[1] - columns
    return pl.pallas_call(
        prepare_kernel,
        out_shape=(jax.ShapeDtypeStruct((points, length), BF16), jax.ShapeDtypeStruct((points, columns), F32)),
        in_specs=[pl.BlockSpec(memory_space=pltpu.SMEM)] + [vmem] * 8,
        out_specs=(vmem, vmem),
        scratch_shapes=[pltpu.VMEM((depth, mine.shape[1]), BF16)],
        compiler_params=pltpu.CompilerParams(vmem_limit_bytes=24 << 20),
        cost_estimate=pl.CostEstimate(flops=1_200_000_000, bytes_accessed=7_000_000, transcendentals=0),
    )(picks, mine, partner, before, after, returned, modes, basis, coeffs)


def close_kernel(pieces, coupling, own, weight, fixed, top, block, interior):
    chips, _, columns, length = pieces.shape
    field = pieces[:, 1].reshape(chips * columns, length).astype(F32).T
    top[...] = field
    rounded = field.astype(BF16)
    block[...] = (own[...] + jnp.dot(coupling[...], rounded, preferred_element_type=F32)).astype(BF16)

    @pl.loop(0, weight.shape[0] // ROWS)
    def _(step):
        rows = pl.ds(pl.multiple_of(step * ROWS, ROWS), ROWS)
        part = jnp.dot(weight[rows, :], rounded, preferred_element_type=F32)
        interior[rows, :] = (fixed[rows, :] + part).astype(BF16)


def close(pieces, coupling, own_block, weight, fixed):
    members, columns, length = pieces.shape
    vmem = pl.BlockSpec(memory_space=pltpu.VMEM)
    return pl.pallas_call(
        close_kernel,
        out_shape=(
            jax.ShapeDtypeStruct((length, members // 2 * columns), F32),
            jax.ShapeDtypeStruct(own_block.shape, BF16),
            jax.ShapeDtypeStruct(fixed.shape, BF16),
        ),
        in_specs=[vmem] * 5,
        out_specs=(vmem, vmem, vmem),
        compiler_params=pltpu.CompilerParams(vmem_limit_bytes=24 << 20),
        cost_estimate=pl.CostEstimate(flops=230_000_000, bytes_accessed=4_000_000, transcendentals=0),
    )(pieces.reshape(members // 2, 2, columns, length), coupling, own_block, weight, fixed)


def body(
    top_basis,
    top_coeffs,
    top_coupling,
    block_coupling,
    block_basis,
    block_coeffs,
    sub_basis,
    sub_coeffs,
    basis_widths,
    constraint_modes,
    adjacency,
):
    chain = lax.axis_size("grp")
    place = lax.axis_index("sub")
    coupling = top_coupling[0]
    high = coupling.astype(BF16)

    basis = spread(top_basis[0]).reshape(-1, top_basis.shape[-1])
    back_1 = along_chain(high, 1, range(2, chain))

    chips = lax.axis_size("sub") // (2 * PARTS)
    columns = top_coeffs.shape[-1] // chips
    coeffs = lax.dynamic_slice_in_dim(top_coeffs[0].T, (place // 2 % chips) * columns, columns, 0)
    own = lax.dot_general(coeffs, basis, (((1,), (1,)), ((), ())), preferred_element_type=F32)

    own_1 = along_chain(own, 1, range(1, chain))
    two, two_a, two_b = advance(coupling, back_1, 2, 0, chain)
    field = own + rows_times(own_1, coupling)

    back_2a = along_chain(two_a, 2, range(LATE, LAST))
    back_2b = along_chain(two_b, 2, range(LAST, chain))
    late_2a = along_chain(field, 2, range(LATE, LAST))
    late_2b = along_chain(field, 2, range(LAST, chain))
    for first in range(2, LATE - 2, 2):
        earlier = along_chain(field, 2, range(first, first + 2))
        field = field + rows_times(earlier, two)
    earlier_4 = along_chain(field, 4, range(LATE, LAST))
    earlier = along_chain(field, 2, range(LATE - 2, LATE))
    late_a = lax.optimization_barrier(rows_times(late_2a, two))
    (four_a,) = advance(two, back_2a, 0, LATE, LAST)
    field = field + late_a + rows_times(earlier, two) + rows_times(earlier_4, four_a)
    earlier = along_chain(field, 4, range(LAST, chain))
    late_b = lax.optimization_barrier(rows_times(late_2b, two))
    (four_b,) = advance(two, back_2b, 0, LAST, chain)
    field = field + late_b + rows_times(earlier, four_b)

    pieces = spread(field.astype(BF16), PARTS)

    own_block = jnp.dot(block_basis[0, 0], block_coeffs[0, 0], preferred_element_type=F32)
    block_high = block_coupling[0, 0].astype(BF16)
    mine = jnp.concatenate([block_high, own_block.astype(BF16)], axis=1)
    partner = swap_cores(mine)
    pair = jnp.stack([mine, partner])
    before = even_along_loop(pair, 2)
    after = even_along_loop(pair, -2)
    both = jnp.concatenate([before, after])
    returned = even_to_odd(both)
    parity = place % 2
    picks = jnp.concatenate([adjacency[0, 0] + parity, basis_widths[0], parity[None]]).astype(jnp.int32)
    weight, fixed = prepare(
        picks,
        mine,
        partner,
        before,
        after,
        returned,
        constraint_modes[0, 0],
        sub_basis[0, 0],
        sub_coeffs[0, 0],
    )
    top_field, block, interior = close(pieces, block_high, own_block, weight, fixed)
    return (top_field[None], block[None, None], interior[None, None])


def solution(mesh):
    placed = (
        P("grp", "sub", None),
        P("grp", None, None),
        P("grp", None, None),
        P("grp", "sub", None, None),
        P("grp", "sub", None, None),
        P("grp", "sub", None, None),
        P("grp", "sub", None, None),
        P("grp", "sub", None, None),
        P("grp", "sub"),
        P("grp", "sub", None, None),
        P("grp", "sub", None),
    )

    return jax.shard_map(
        body,
        mesh=mesh,
        in_specs=placed,
        out_specs=(P("grp", None, None), P("grp", "sub", None, None), P("grp", "sub", None, None)),
        check_vma=False,
    )
```

```python
import functools

import jax
import jax.numpy as jnp
from jax import lax
from jax.experimental import pallas as pl
from jax.experimental.pallas import tpu as pltpu
from jax.sharding import PartitionSpec as P


BF16 = jnp.bfloat16
F32 = jnp.float32
ROWS = 256
LATE = 10
LAST = 12
PARTS = 2


def spread(piece, parts=1):
    peers = lax.axis_size("sub") // parts
    copies = jnp.broadcast_to(piece[None], (peers,) + piece.shape)
    groups = [list(range(part * peers, (part + 1) * peers)) for part in range(parts)]
    return lax.all_to_all(copies, "sub", 0, 0, axis_index_groups=groups if parts > 1 else None)


def along_chain(value, by, groups):
    peers = lax.axis_size("sub")
    pairs = [((g - by) * peers + s, g * peers + s) for g in groups if g >= by for s in range(1, peers, 2)]
    return lax.ppermute(value, ("grp", "sub"), pairs)


def swap_cores(value):
    peers = lax.axis_size("sub")
    return lax.ppermute(value, "sub", [(i, i ^ 1) for i in range(peers)])


def even_along_loop(value, by):
    peers = lax.axis_size("sub")
    return lax.ppermute(value, "sub", [(i, (i + by) % peers) for i in range(0, peers, 2)])


def even_to_odd(value):
    peers = lax.axis_size("sub")
    return lax.ppermute(value, "sub", [(i, i + 1) for i in range(0, peers, 2)])


def in_groups(first, last):
    group = lax.axis_index("grp")
    return (group >= first) & (group < last)


def step_kernel(first, last, base, value, left, out):
    used = in_groups(first, last)
    dims = (((1,), (1,)), ((), ()))

    @pl.when(used)
    def _():
        whole = value[...]
        count = whole.shape[0]
        top = whole.astype(BF16)
        both = jnp.concatenate([top, (whole - top.astype(F32)).astype(BF16)])
        high = left[...].astype(BF16)
        low = (left[...] - high.astype(F32)).astype(BF16)
        far = lax.dot_general(both, high, dims, preferred_element_type=F32)
        near = lax.dot_general(top, low, dims, preferred_element_type=F32)
        out[...] = base[...] + far[:count] + far[count:] + near

    @pl.when(jnp.logical_not(used))
    def _():
        out[...] = base[...]


def add_step(base, value, left, first, last):
    vmem = pl.BlockSpec(memory_space=pltpu.VMEM)
    return pl.pallas_call(
        functools.partial(step_kernel, first, last),
        out_shape=jax.ShapeDtypeStruct(base.shape, F32),
        in_specs=[vmem] * 3,
        out_specs=vmem,
        compiler_params=pltpu.CompilerParams(vmem_limit_bytes=8 << 20),
        cost_estimate=pl.CostEstimate(flops=25_000_000, bytes_accessed=1_200_000, transcendentals=0),
    )(base, value, left)


def advance_kernel(first, last, left, right, product, *rounded):
    steps = left.shape[0] // ROWS
    if first:
        group = lax.axis_index("grp")
        used = (group >= first) & (group < last)

        @pl.when(jnp.logical_not(used))
        def _():
            product[...] = jnp.zeros(product.shape, F32)

        steps = jnp.where(used, steps, 0)

    @pl.loop(0, steps)
    def _(step):
        rows = pl.ds(pl.multiple_of(step * ROWS, ROWS), ROWS)
        whole = left[rows, :]
        high = whole.astype(BF16)
        low = (whole - high.astype(F32)).astype(BF16)
        result = jnp.dot(high, right[...], preferred_element_type=F32)
        result = result + jnp.dot(low, right[...], preferred_element_type=F32)
        product[rows, :] = result
        for out in rounded:
            out[rows, :] = result.astype(BF16)


def advance(left, right, copies, first, last):
    vmem = pl.BlockSpec(memory_space=pltpu.VMEM)
    return pl.pallas_call(
        functools.partial(advance_kernel, first, last),
        out_shape=[jax.ShapeDtypeStruct(left.shape, F32)] + [jax.ShapeDtypeStruct(left.shape, BF16)] * copies,
        in_specs=[vmem] * 2,
        out_specs=[vmem] * (1 + copies),
        compiler_params=pltpu.CompilerParams(vmem_limit_bytes=8 << 20),
        cost_estimate=pl.CostEstimate(flops=540_000_000, bytes_accessed=3_000_000, transcendentals=0),
    )(left, right)


def rows_times(value, left):
    dims = (((1,), (1,)), ((), ()))
    return lax.dot_general(value, left, dims, precision=lax.Precision.HIGH, preferred_element_type=F32)


def prepare_kernel(picks, mine, partner, before, after, returned, modes, basis, coeffs, weight, fixed, linked):
    size = mine.shape[0]
    length = weight.shape[1]
    parity = picks[5]
    for slot in range(4):
        pick = picks[slot]
        rows = pl.ds(slot * size, size)

        @pl.when(pick < 2)
        def _():
            linked[rows, :] = before[pick] + returned[pick]

        @pl.when(pick == parity + 2)
        def _():
            linked[rows, :] = mine[...]

        @pl.when(pick == 3 - parity)
        def _():
            linked[rows, :] = partner[...]

        @pl.when(pick > 3)
        def _():
            linked[rows, :] = after[pick - 4] + returned[pick - 2]

    live = lax.broadcasted_iota(jnp.int32, coeffs.shape, 0) < picks[4]
    kept = jnp.where(live, coeffs[...], jnp.zeros(coeffs.shape, coeffs.dtype))

    @pl.loop(0, modes.shape[0] // ROWS)
    def _(step):
        rows = pl.ds(pl.multiple_of(step * ROWS, ROWS), ROWS)
        both = jnp.dot(modes[rows, :], linked[...], preferred_element_type=F32)
        weight[rows, :] = both[:, :length].astype(BF16)
        fixed[rows, :] = both[:, length:] + jnp.dot(basis[rows, :], kept, preferred_element_type=F32)


def prepare(picks, mine, partner, before, after, returned, modes, basis, coeffs):
    vmem = pl.BlockSpec(memory_space=pltpu.VMEM)
    points, depth = modes.shape
    columns = coeffs.shape[1]
    length = mine.shape[1] - columns
    return pl.pallas_call(
        prepare_kernel,
        out_shape=(jax.ShapeDtypeStruct((points, length), BF16), jax.ShapeDtypeStruct((points, columns), F32)),
        in_specs=[pl.BlockSpec(memory_space=pltpu.SMEM)] + [vmem] * 8,
        out_specs=(vmem, vmem),
        scratch_shapes=[pltpu.VMEM((depth, mine.shape[1]), BF16)],
        compiler_params=pltpu.CompilerParams(vmem_limit_bytes=24 << 20),
        cost_estimate=pl.CostEstimate(flops=1_200_000_000, bytes_accessed=7_000_000, transcendentals=0),
    )(picks, mine, partner, before, after, returned, modes, basis, coeffs)


def close_kernel(pieces, coupling, own, weight, fixed, top_hbm, block_hbm, interior_hbm, top, block, interior, done):
    chips, _, columns, length = pieces.shape
    field = pieces[:, 1].reshape(chips * columns, length).astype(F32).T
    top[...] = field
    stores = [pltpu.make_async_copy(top, top_hbm, done.at[0])]
    stores[0].start()
    rounded = field.astype(BF16)
    steps = weight.shape[0] // ROWS
    for step in range(steps):
        rows = pl.ds(step * ROWS, ROWS)
        part = jnp.dot(weight[rows, :], rounded, preferred_element_type=F32)
        interior[rows, :] = (fixed[rows, :] + part).astype(BF16)
        stores.append(pltpu.make_async_copy(interior.at[rows, :], interior_hbm.at[rows, :], done.at[2 + step]))
        stores[-1].start()
    block[...] = (own[...] + jnp.dot(coupling[...], rounded, preferred_element_type=F32)).astype(BF16)
    stores.append(pltpu.make_async_copy(block, block_hbm, done.at[1]))
    stores[-1].start()
    for store in stores:
        store.wait()


def close(pieces, coupling, own_block, weight, fixed):
    members, columns, length = pieces.shape
    vmem = pl.BlockSpec(memory_space=pltpu.VMEM)
    return pl.pallas_call(
        close_kernel,
        out_shape=(
            jax.ShapeDtypeStruct((length, members // 2 * columns), F32),
            jax.ShapeDtypeStruct(own_block.shape, BF16),
            jax.ShapeDtypeStruct(fixed.shape, BF16),
        ),
        in_specs=[vmem] * 5,
        out_specs=[pl.BlockSpec(memory_space=pl.ANY)] * 3,
        scratch_shapes=[
            pltpu.VMEM((length, members // 2 * columns), F32),
            pltpu.VMEM(own_block.shape, BF16),
            pltpu.VMEM(fixed.shape, BF16),
            pltpu.SemaphoreType.DMA((2 + fixed.shape[0] // ROWS,)),
        ],
        compiler_params=pltpu.CompilerParams(vmem_limit_bytes=24 << 20),
        cost_estimate=pl.CostEstimate(flops=230_000_000, bytes_accessed=4_000_000, transcendentals=0),
    )(pieces.reshape(members // 2, 2, columns, length), coupling, own_block, weight, fixed)


def body(
    top_basis,
    top_coeffs,
    top_coupling,
    block_coupling,
    block_basis,
    block_coeffs,
    sub_basis,
    sub_coeffs,
    basis_widths,
    constraint_modes,
    adjacency,
):
    chain = lax.axis_size("grp")
    place = lax.axis_index("sub")
    coupling = top_coupling[0]
    high = coupling.astype(BF16)

    basis = spread(top_basis[0]).reshape(-1, top_basis.shape[-1])
    back_1 = along_chain(high, 1, range(2, chain))

    chips = lax.axis_size("sub") // (2 * PARTS)
    columns = top_coeffs.shape[-1] // chips
    coeffs = lax.dynamic_slice_in_dim(top_coeffs[0].T, (place // 2 % chips) * columns, columns, 0)
    own = lax.dot_general(coeffs, basis, (((1,), (1,)), ((), ())), preferred_element_type=F32)

    own_1 = along_chain(own, 1, range(1, chain))
    two, two_a, two_b = advance(coupling, back_1, 2, 0, chain)
    field = own + rows_times(own_1, coupling)

    back_2a = along_chain(two_a, 2, range(LATE, LAST))
    back_2b = along_chain(two_b, 2, range(LAST, chain))
    late_2a = along_chain(field, 2, range(LATE, LAST))
    late_2b = along_chain(field, 2, range(LAST, chain))
    for first in range(2, LATE - 2, 2):
        earlier = along_chain(field, 2, range(first, first + 2))
        field = add_step(field, earlier, two, first, first + 2)
    earlier_4 = along_chain(field, 4, range(LATE, LAST))
    earlier = along_chain(field, 2, range(LATE - 2, LATE))
    field = add_step(field, late_2a, two, LATE, LAST)
    (four_a,) = advance(two, back_2a, 0, LATE, LAST)
    field = add_step(field, earlier, two, LATE - 2, LATE)
    field = add_step(field, earlier_4, four_a, LATE, LAST)
    earlier = along_chain(field, 4, range(LAST, chain))
    field = add_step(field, late_2b, two, LAST, chain)
    (four_b,) = advance(two, back_2b, 0, LAST, chain)
    field = add_step(field, earlier, four_b, LAST, chain)

    pieces = spread(field.astype(BF16), PARTS)

    own_block = jnp.dot(block_basis[0, 0], block_coeffs[0, 0], preferred_element_type=F32)
    block_high = block_coupling[0, 0].astype(BF16)
    mine = jnp.concatenate([block_high, own_block.astype(BF16)], axis=1)
    partner = swap_cores(mine)
    pair = jnp.stack([mine, partner])
    before = even_along_loop(pair, 2)
    after = even_along_loop(pair, -2)
    both = jnp.concatenate([before, after])
    returned = even_to_odd(both)
    parity = place % 2
    picks = jnp.concatenate([adjacency[0, 0] + parity, basis_widths[0], parity[None]]).astype(jnp.int32)
    weight, fixed = prepare(
        picks,
        mine,
        partner,
        before,
        after,
        returned,
        constraint_modes[0, 0],
        sub_basis[0, 0],
        sub_coeffs[0, 0],
    )
    top_field, block, interior = close(pieces, block_high, own_block, weight, fixed)
    return (top_field[None], block[None, None], interior[None, None])


def solution(mesh):
    placed = (
        P("grp", "sub", None),
        P("grp", None, None),
        P("grp", None, None),
        P("grp", "sub", None, None),
        P("grp", "sub", None, None),
        P("grp", "sub", None, None),
        P("grp", "sub", None, None),
        P("grp", "sub", None, None),
        P("grp", "sub"),
        P("grp", "sub", None, None),
        P("grp", "sub", None),
    )

    return jax.shard_map(
        body,
        mesh=mesh,
        in_specs=placed,
        out_specs=(P("grp", None, None), P("grp", "sub", None, None), P("grp", "sub", None, None)),
        check_vma=False,
    )
```

```python
import functools

import jax
import jax.numpy as jnp
from jax import lax
from jax.experimental import pallas as pl
from jax.experimental.pallas import tpu as pltpu
from jax.sharding import PartitionSpec as P


BF16 = jnp.bfloat16
F32 = jnp.float32
ROWS = 256
LATE = 10
LAST = 12
PARTS = 2


def spread(piece, parts=1):
    peers = lax.axis_size("sub") // parts
    copies = jnp.broadcast_to(piece[None], (peers,) + piece.shape)
    groups = [list(range(part * peers, (part + 1) * peers)) for part in range(parts)]
    return lax.all_to_all(copies, "sub", 0, 0, axis_index_groups=groups if parts > 1 else None)


def along_chain(value, by, groups):
    peers = lax.axis_size("sub")
    pairs = [((g - by) * peers + s, g * peers + s) for g in groups if g >= by for s in range(1, peers, 2)]
    return lax.ppermute(value, ("grp", "sub"), pairs)


def swap_cores(value):
    peers = lax.axis_size("sub")
    return lax.ppermute(value, "sub", [(i, i ^ 1) for i in range(peers)])


def even_along_loop(value, by):
    peers = lax.axis_size("sub")
    return lax.ppermute(value, "sub", [(i, (i + by) % peers) for i in range(0, peers, 2)])


def even_to_odd(value):
    peers = lax.axis_size("sub")
    return lax.ppermute(value, "sub", [(i, i + 1) for i in range(0, peers, 2)])


def in_groups(first, last):
    group = lax.axis_index("grp")
    return (group >= first) & (group < last)


def step_kernel(first, last, base, value, left, out):
    used = in_groups(first, last)
    dims = (((1,), (1,)), ((), ()))

    @pl.when(used)
    def _():
        whole = value[...]
        count = whole.shape[0]
        top = whole.astype(BF16)
        both = jnp.concatenate([top, (whole - top.astype(F32)).astype(BF16)])
        high = left[...].astype(BF16)
        low = (left[...] - high.astype(F32)).astype(BF16)
        far = lax.dot_general(both, high, dims, preferred_element_type=F32)
        near = lax.dot_general(top, low, dims, preferred_element_type=F32)
        out[...] = base[...] + far[:count] + far[count:] + near

    @pl.when(jnp.logical_not(used))
    def _():
        out[...] = base[...]


def add_step(base, value, left, first, last):
    vmem = pl.BlockSpec(memory_space=pltpu.VMEM)
    return pl.pallas_call(
        functools.partial(step_kernel, first, last),
        out_shape=jax.ShapeDtypeStruct(base.shape, F32),
        in_specs=[vmem] * 3,
        out_specs=vmem,
        compiler_params=pltpu.CompilerParams(vmem_limit_bytes=8 << 20),
        cost_estimate=pl.CostEstimate(flops=25_000_000, bytes_accessed=1_200_000, transcendentals=0),
    )(base, value, left)


def advance_kernel(first, last, left, right, product, *rounded):
    steps = left.shape[0] // ROWS
    if first:
        group = lax.axis_index("grp")
        used = (group >= first) & (group < last)

        @pl.when(jnp.logical_not(used))
        def _():
            product[...] = jnp.zeros(product.shape, F32)

        steps = jnp.where(used, steps, 0)

    @pl.loop(0, steps)
    def _(step):
        rows = pl.ds(pl.multiple_of(step * ROWS, ROWS), ROWS)
        whole = left[rows, :]
        high = whole.astype(BF16)
        low = (whole - high.astype(F32)).astype(BF16)
        result = jnp.dot(high, right[...], preferred_element_type=F32)
        result = result + jnp.dot(low, right[...], preferred_element_type=F32)
        product[rows, :] = result
        for out in rounded:
            out[rows, :] = result.astype(BF16)


def advance(left, right, copies, first, last):
    vmem = pl.BlockSpec(memory_space=pltpu.VMEM)
    return pl.pallas_call(
        functools.partial(advance_kernel, first, last),
        out_shape=[jax.ShapeDtypeStruct(left.shape, F32)] + [jax.ShapeDtypeStruct(left.shape, BF16)] * copies,
        in_specs=[vmem] * 2,
        out_specs=[vmem] * (1 + copies),
        compiler_params=pltpu.CompilerParams(vmem_limit_bytes=8 << 20),
        cost_estimate=pl.CostEstimate(flops=540_000_000, bytes_accessed=3_000_000, transcendentals=0),
    )(left, right)


def rows_times(value, left):
    dims = (((1,), (1,)), ((), ()))
    return lax.dot_general(value, left, dims, precision=lax.Precision.HIGH, preferred_element_type=F32)


def prepare_kernel(picks, mine, partner, before, after, returned, modes, basis, coeffs, weight, fixed, linked):
    size = mine.shape[0]
    length = weight.shape[1]
    parity = picks[5]
    for slot in range(4):
        pick = picks[slot]
        rows = pl.ds(slot * size, size)

        @pl.when(pick < 2)
        def _():
            linked[rows, :] = before[pick] + returned[pick]

        @pl.when(pick == parity + 2)
        def _():
            linked[rows, :] = mine[...]

        @pl.when(pick == 3 - parity)
        def _():
            linked[rows, :] = partner[...]

        @pl.when(pick > 3)
        def _():
            linked[rows, :] = after[pick - 4] + returned[pick - 2]

    live = lax.broadcasted_iota(jnp.int32, coeffs.shape, 0) < picks[4]
    kept = jnp.where(live, coeffs[...], jnp.zeros(coeffs.shape, coeffs.dtype))

    @pl.loop(0, modes.shape[0] // ROWS)
    def _(step):
        rows = pl.ds(pl.multiple_of(step * ROWS, ROWS), ROWS)
        both = jnp.dot(modes[rows, :], linked[...], preferred_element_type=F32)
        weight[rows, :] = both[:, :length].astype(BF16)
        fixed[rows, :] = both[:, length:] + jnp.dot(basis[rows, :], kept, preferred_element_type=F32)


def prepare(picks, mine, partner, before, after, returned, modes, basis, coeffs):
    vmem = pl.BlockSpec(memory_space=pltpu.VMEM)
    points, depth = modes.shape
    columns = coeffs.shape[1]
    length = mine.shape[1] - columns
    return pl.pallas_call(
        prepare_kernel,
        out_shape=(jax.ShapeDtypeStruct((points, length), BF16), jax.ShapeDtypeStruct((points, columns), F32)),
        in_specs=[pl.BlockSpec(memory_space=pltpu.SMEM)] + [vmem] * 8,
        out_specs=(vmem, vmem),
        scratch_shapes=[pltpu.VMEM((depth, mine.shape[1]), BF16)],
        compiler_params=pltpu.CompilerParams(vmem_limit_bytes=24 << 20),
        cost_estimate=pl.CostEstimate(flops=1_200_000_000, bytes_accessed=7_000_000, transcendentals=0),
    )(picks, mine, partner, before, after, returned, modes, basis, coeffs)


def close_kernel(pieces, coupling, own, weight, fixed, top_hbm, block_hbm, interior_hbm, top, block, interior, done):
    chips, _, columns, length = pieces.shape
    field = pieces[:, 1].reshape(chips * columns, length).astype(F32).T
    top[...] = field
    stores = [pltpu.make_async_copy(top, top_hbm, done.at[0])]
    stores[0].start()
    rounded = field.astype(BF16)
    steps = weight.shape[0] // ROWS
    for step in range(steps):
        rows = pl.ds(step * ROWS, ROWS)
        part = jnp.dot(weight[rows, :], rounded, preferred_element_type=F32)
        interior[rows, :] = (fixed[rows, :] + part).astype(BF16)
        stores.append(pltpu.make_async_copy(interior.at[rows, :], interior_hbm.at[rows, :], done.at[2 + step]))
        stores[-1].start()
    block[...] = (own[...] + jnp.dot(coupling[...], rounded, preferred_element_type=F32)).astype(BF16)
    stores.append(pltpu.make_async_copy(block, block_hbm, done.at[1]))
    stores[-1].start()
    for store in stores:
        store.wait()


def close(pieces, coupling, own_block, weight, fixed):
    members, columns, length = pieces.shape
    vmem = pl.BlockSpec(memory_space=pltpu.VMEM)
    return pl.pallas_call(
        close_kernel,
        out_shape=(
            jax.ShapeDtypeStruct((length, members // 2 * columns), F32),
            jax.ShapeDtypeStruct(own_block.shape, BF16),
            jax.ShapeDtypeStruct(fixed.shape, BF16),
        ),
        in_specs=[vmem] * 5,
        out_specs=[pl.BlockSpec(memory_space=pl.ANY)] * 3,
        scratch_shapes=[
            pltpu.VMEM((length, members // 2 * columns), F32),
            pltpu.VMEM(own_block.shape, BF16),
            pltpu.VMEM(fixed.shape, BF16),
            pltpu.SemaphoreType.DMA((2 + fixed.shape[0] // ROWS,)),
        ],
        compiler_params=pltpu.CompilerParams(vmem_limit_bytes=24 << 20),
        cost_estimate=pl.CostEstimate(flops=230_000_000, bytes_accessed=4_000_000, transcendentals=0),
    )(pieces.reshape(members // 2, 2, columns, length), coupling, own_block, weight, fixed)


def body(
    top_basis,
    top_coeffs,
    top_coupling,
    block_coupling,
    block_basis,
    block_coeffs,
    sub_basis,
    sub_coeffs,
    basis_widths,
    constraint_modes,
    adjacency,
):
    chain = lax.axis_size("grp")
    place = lax.axis_index("sub")
    coupling = top_coupling[0]
    high = coupling.astype(BF16)

    basis = spread(top_basis[0]).reshape(-1, top_basis.shape[-1])
    back_1 = along_chain(high, 1, range(2, chain))

    chips = lax.axis_size("sub") // (2 * PARTS)
    columns = top_coeffs.shape[-1] // chips
    coeffs = lax.dynamic_slice_in_dim(top_coeffs[0].T, (place // 2 % chips) * columns, columns, 0)
    own = lax.dot_general(coeffs, basis, (((1,), (1,)), ((), ())), preferred_element_type=F32)

    own_1 = along_chain(own, 1, range(1, chain))
    two, two_a, two_b = advance(coupling, back_1, 2, 0, chain)
    field = own + rows_times(own_1, coupling)

    back_2a = along_chain(two_a, 2, range(LATE, LAST))
    back_2b = along_chain(two_b, 2, range(LAST, chain))
    late_2a = along_chain(field, 2, range(LATE, LAST))
    late_2b = along_chain(field, 2, range(LAST, chain))
    for first in range(2, LATE - 2, 2):
        earlier = along_chain(field, 2, range(first, first + 2))
        field = add_step(field, earlier, two, first, first + 2)
    earlier_4 = along_chain(field, 4, range(LATE, LAST))
    earlier = along_chain(field, 2, range(LATE - 2, LATE))
    field = field + rows_times(late_2a, two)
    (four_a,) = advance(two, back_2a, 0, LATE, LAST)
    field = field + rows_times(earlier, two)
    field = field + rows_times(earlier_4, four_a)
    earlier = along_chain(field, 4, range(LAST, chain))
    field = add_step(field, late_2b, two, LAST, chain)
    (four_b,) = advance(two, back_2b, 0, LAST, chain)
    field = add_step(field, earlier, four_b, LAST, chain)

    pieces = spread(field.astype(BF16), PARTS)

    own_block = jnp.dot(block_basis[0, 0], block_coeffs[0, 0], preferred_element_type=F32)
    block_high = block_coupling[0, 0].astype(BF16)
    mine = jnp.concatenate([block_high, own_block.astype(BF16)], axis=1)
    partner = swap_cores(mine)
    pair = jnp.stack([mine, partner])
    before = even_along_loop(pair, 2)
    after = even_along_loop(pair, -2)
    both = jnp.concatenate([before, after])
    returned = even_to_odd(both)
    parity = place % 2
    picks = jnp.concatenate([adjacency[0, 0] + parity, basis_widths[0], parity[None]]).astype(jnp.int32)
    weight, fixed = prepare(
        picks,
        mine,
        partner,
        before,
        after,
        returned,
        constraint_modes[0, 0],
        sub_basis[0, 0],
        sub_coeffs[0, 0],
    )
    top_field, block, interior = close(pieces, block_high, own_block, weight, fixed)
    return (top_field[None], block[None, None], interior[None, None])


def solution(mesh):
    placed = (
        P("grp", "sub", None),
        P("grp", None, None),
        P("grp", None, None),
        P("grp", "sub", None, None),
        P("grp", "sub", None, None),
        P("grp", "sub", None, None),
        P("grp", "sub", None, None),
        P("grp", "sub", None, None),
        P("grp", "sub"),
        P("grp", "sub", None, None),
        P("grp", "sub", None),
    )

    return jax.shard_map(
        body,
        mesh=mesh,
        in_specs=placed,
        out_specs=(P("grp", None, None), P("grp", "sub", None, None), P("grp", "sub", None, None)),
        check_vma=False,
    )
```
